32 devices in a mesh: arc: 16 (over z, x, core), ord: 2 (over y).
Axes of the slice: x: 2, y: 2, z: 4, core: 2. Of those that a mesh axis runs over, the one named last changes fastest.
Arguments:
- design: bfloat16 [16384, 32768], P('arc', 'ord'), may hold values from -4 to 4
- arc_lengths: int32 [16], P('arc'), may hold values from 1 to 1024, 10240 in all
- kaula_prior: float32 [1024], replicated, may hold values from 1 to 20
Outputs:
- factor: float32 [1024, 32768], P('arc', 'ord')
The draws below stay inside these ranges and needn't reach their ends.
Inputs may be any that keep to these rules, and one draw needn't show every extreme that they name: `arc_lengths`: some arc has all 1024 slots live.
All inputs are finite; a program needn't handle non-finite values. No bound on the sum of `arc_lengths` on one device may be relied on, other than what follows from the above.
Results may differ from the reference program's by a relative error of at most 0.0003.
Values may be sent and summed in bfloat16 or wider, within the bound.
A program may use at most 320 MiB of HBM per device.

```python
import math
import jax
import jax.numpy as jnp
import numpy as np
from jax import lax

TILE = 512
PANELS = 2
COEFFS = 32768
STEPS = 1024
SLAB = 1024
ARCS = 16
OBSERVATIONS = 16384


def draw_design(key, part):
    taps = 8
    wide = COEFFS + taps - 1
    scale_back = 1.0 / math.sqrt(12.0)

    def one_block(index):
        sub = jax.random.fold_in(key, index)
        first_key, second_key = jax.random.split(sub)
        source = jax.random.normal(first_key, (STEPS, wide), jnp.float32)
        white = jax.random.normal(second_key, (STEPS, COEFFS), jnp.float32)
        total = source[:, 0:COEFFS]
        for shift in range(1, taps):
            total = total + source[:, shift:shift + COEFFS]
        total = total + 2.0 * white
        return jnp.clip(total * scale_back, -4.0, 4.0).astype(jnp.bfloat16)
    blocks = lax.map(one_block, jnp.arange(ARCS, dtype=jnp.int32))
    return blocks.reshape(OBSERVATIONS, COEFFS)


def length_profile(amount, total, limit, slope):
    loads = [(1 << 20) // math.isqrt(grade ** slope) + 1 for grade in range(2, amount + 1)]
    surplus, holding = total - limit - (amount - 1), [1] * (amount - 1)
    while surplus > 0:
        free = [i for i in range(amount - 1) if holding[i] < limit]
        pool, left = sum([loads[i] for i in free]), surplus
        for i in free:
            more = min(limit - holding[i], max(1, left * loads[i] // pool), surplus)
            holding[i] = holding[i] + more
            surplus = surplus - more
    return np.array([limit] + holding)


def uneven(key, amount, total, bound, lean):
    if amount == 2:
        one = jax.random.randint(key, (), max(1, total - bound), min(bound, total - 1) + 1)
        return jnp.stack([one, total - one])
    sizes = jnp.asarray(length_profile(amount, total, bound, lean), jnp.int32)
    twos = (amount - 1) // 2
    giver, receiver = sizes[1:1 + 2 * twos:2], sizes[2:2 + 2 * twos:2]
    room = jnp.minimum(giver - 1, bound - receiver)
    passed = jax.random.randint(jax.random.fold_in(key, 1), (twos,), 0, 1 << 20) % (room + 1)
    sizes = sizes.at[1:1 + 2 * twos:2].set(giver - passed).at[2:2 + 2 * twos:2].set(receiver + passed)
    return sizes[jax.random.permutation(jax.random.fold_in(key, 2), amount)]


def setup_inputs(seed: int = 0) -> dict:
    key_of = jax.random.split(jax.random.key(seed), 4)
    design = draw_design(jax.random.fold_in(key_of[3], 71), 0)
    arc_lengths = uneven(key_of[1], ARCS, ARCS * STEPS * 5 // 8, STEPS, 2).astype(jnp.int32)
    kaula_prior = jnp.clip(jnp.exp(jax.random.uniform(key_of[2], (SLAB,), jnp.float32, math.log(1.0), math.log(20.0))), 1.0, 20.0)
    return dict(design=design, arc_lengths=arc_lengths, kaula_prior=kaula_prior)


def reference(design, arc_lengths, kaula_prior):
    total_rows = design.shape[0]
    row_ids = jnp.arange(total_rows, dtype=jnp.int32)
    arc_of = (row_ids // STEPS).astype(jnp.int32)
    in_arc = row_ids % STEPS
    is_live = in_arc < arc_lengths[arc_of]
    masked = jnp.where(is_live[:, None], design[:, :SLAB], jnp.zeros((), design.dtype))
    normal = jnp.dot(masked.T.astype(jnp.float32), design.astype(jnp.float32), preferred_element_type=jnp.float32) * (1.0 / math.sqrt(OBSERVATIONS))
    diag_ids = jnp.arange(SLAB, dtype=jnp.int32)
    normal = normal.at[diag_ids, diag_ids].add(kaula_prior)
    blocks = [normal[p * TILE:(p + 1) * TILE] for p in range(PANELS)]
    for p in range(PANELS):
        lower_factor = jnp.linalg.cholesky(blocks[p][:, p * TILE:(p + 1) * TILE])
        blocks[p] = jax.scipy.linalg.solve_triangular(lower_factor, blocks[p], lower=True)
        for q in range(p + 1, PANELS):
            upper_tile = blocks[p][:, q * TILE:(q + 1) * TILE]
            blocks[q] = blocks[q] - jnp.dot(upper_tile.T, blocks[p], precision=lax.Precision.HIGHEST)
    return jnp.concatenate(blocks, axis=0)
```

```python
import math

import jax
import jax.numpy as jnp
from jax import lax
from jax.experimental import pallas as pl
from jax.experimental.pallas import tpu as pltpu
from jax.sharding import PartitionSpec as P

TILE = 512
PANELS = 2


def broadcast(block, axis, source):
    block = jnp.where(lax.axis_index(axis) == source, block, jnp.zeros_like(block))
    return lax.psum(block, axis)


def apply_panels(matrix, lowers, couplings):
    blocks = [matrix[p * TILE : (p + 1) * TILE] for p in range(PANELS)]
    for p in range(PANELS):
        blocks[p] = jax.scipy.linalg.solve_triangular(lowers[p], blocks[p], lower=True)
        for q in range(p + 1, PANELS):
            blocks[q] = blocks[q] - jnp.dot(
                couplings[p, q].T, blocks[p], precision=lax.Precision.HIGHEST
            )
    return jnp.concatenate(blocks, axis=0)


def on_device(design, arc_lengths, kaula_prior):
    obs_dev, ord_cols = design.shape
    arcs_here = arc_lengths.shape[0]
    arc_steps = obs_dev // arcs_here
    row_block = min(256, arc_steps)
    slab_rows = TILE * PANELS
    pieces = []
    for panel_index in range(PANELS):
        owner = panel_index * TILE // ord_cols
        offset = panel_index * TILE % ord_cols
        piece = design[:, offset : offset + TILE]
        pieces.append(broadcast(piece, "ord", owner))
    slab_cols = jnp.concatenate(pieces, axis=1)
    position = lax.broadcasted_iota(jnp.int32, (row_block, 1), 0)
    partial_value = jnp.zeros((slab_rows, ord_cols), jnp.float32)
    gram_part = jnp.zeros((slab_rows, slab_rows), jnp.float32)
    arc_slot = 0
    length = arc_lengths[arc_slot]
    blocks_live = (length + row_block - 1) // row_block

    def accumulate(step_idx, running, arc_slot=arc_slot, length=length):
        first_row = arc_slot * arc_steps + step_idx * row_block
        slab_block = lax.dynamic_slice_in_dim(slab_cols, first_row, row_block, 0)
        tile_block = lax.dynamic_slice_in_dim(design, first_row, row_block, 0)
        is_live = position + step_idx * row_block < length
        live_block = jnp.where(is_live, slab_block, jnp.zeros((), slab_block.dtype))
        dims = (((0,), (0,)), ((), ()))
        normal_acc = running[0] + lax.dot_general(
            live_block, tile_block, dims, preferred_element_type=jnp.float32
        )
        gram_acc = running[1] + lax.dot_general(
            live_block, slab_block, dims, preferred_element_type=jnp.float32
        )
        return (normal_acc, gram_acc)

    partial_value, gram_part = lax.fori_loop(0, blocks_live, accumulate, (partial_value, gram_part))
    inverse_norm = 1.0 / math.sqrt(lax.axis_size("arc") * obs_dev)
    square_ids = lax.broadcasted_iota(jnp.int32, (slab_rows, slab_rows), 0)
    square_cols = lax.broadcasted_iota(jnp.int32, (slab_rows, slab_rows), 1)
    gram = lax.psum(gram_part, "arc") * inverse_norm
    gram = gram + jnp.where(square_ids == square_cols, kaula_prior[:, None], 0.0)
    gram_blocks = [gram[p * TILE : (p + 1) * TILE] for p in range(PANELS)]
    lowers = []
    couplings = {}
    for p in range(PANELS):
        lower_factor = jnp.linalg.cholesky(gram_blocks[p][:, p * TILE : (p + 1) * TILE])
        lowers.append(lower_factor)
        gram_blocks[p] = jax.scipy.linalg.solve_triangular(lower_factor, gram_blocks[p], lower=True)
        for q in range(p + 1, PANELS):
            upper_tile = gram_blocks[p][:, q * TILE : (q + 1) * TILE]
            couplings[p, q] = upper_tile
            gram_blocks[q] = gram_blocks[q] - jnp.dot(
                upper_tile.T, gram_blocks[p], precision=lax.Precision.HIGHEST
            )
    row_index = lax.broadcasted_iota(jnp.int32, (slab_rows, 1), 0)
    summed = lax.psum_scatter(partial_value, "arc", scatter_dimension=1, tiled=True) * inverse_norm
    width = ord_cols // lax.axis_size("arc")
    col_first = lax.axis_index("ord") * ord_cols + lax.axis_index("arc") * width
    global_col = col_first + lax.broadcasted_iota(jnp.int32, (1, width), 1)
    matrix = summed + jnp.where(row_index == global_col, kaula_prior[:, None], 0.0)
    share = apply_panels(matrix, lowers, couplings)
    factor = lax.all_to_all(share, "arc", split_axis=0, concat_axis=1, tiled=True)
    return factor


NB = 128
GROUP = 128
LEVELS = 32767.0


def diagonal_inverse(block):
    tiles = NB // 8
    sub = lax.broadcasted_iota(jnp.int32, (8, NB), 0)
    lane = lax.broadcasted_iota(jnp.int32, (8, NB), 1)
    rest = [block[8 * t : 8 * t + 8] for t in range(tiles)]
    inv = [jnp.where(sub + 8 * t == lane, 1.0, 0.0).astype(jnp.float32) for t in range(tiles)]
    for j in range(NB):
        t, s = j // 8, j % 8
        column = [jnp.broadcast_to(rest[i][:, j : j + 1], (8, NB)) for i in range(t, tiles)]
        recip = 1.0 / jnp.broadcast_to(column[0][s : s + 1], (8, NB))
        row = jnp.broadcast_to(rest[t][s : s + 1], (8, NB)) * recip
        inv_row = jnp.broadcast_to(inv[t][s : s + 1], (8, NB)) * recip
        for i in range(t, tiles):
            c = column[i - t]
            if i == t:
                c = jnp.where(sub > s, c, 0.0)
            rest[i] = rest[i] - c * row
            inv[i] = inv[i] - c * inv_row
    for t in range(tiles):
        pivot = jnp.sum(jnp.where(sub + 8 * t == lane, rest[t], 0.0), axis=1, keepdims=True)
        inv[t] = inv[t] * (1.0 / jnp.sqrt(pivot))
    return jnp.concatenate(inv, axis=0)


def cholesky_inverse_kernel(gram_ref, out_ref, work, left, right):
    size = gram_ref.shape[0]
    blocks = size // NB
    work[...] = gram_ref[...]
    rows = lax.broadcasted_iota(jnp.int32, (NB, size), 0)
    cols = lax.broadcasted_iota(jnp.int32, (NB, size), 1)
    for i in range(blocks):
        out_ref[i * NB : (i + 1) * NB, :] = jnp.where(rows + i * NB == cols, 1.0, 0.0)

    def step(k, carry):
        first = pl.multiple_of(k * NB, NB)
        here = pl.ds(first, NB)
        inverse = diagonal_inverse(work[here, here])
        left[...] = jnp.dot(inverse, work[here, :], precision=lax.Precision.HIGHEST)
        right[...] = jnp.dot(inverse, out_ref[here, :], precision=lax.Precision.HIGHEST)
        out_ref[here, :] = right[...]

        def update(i, carry):
            there = pl.ds(pl.multiple_of(i * NB, NB), NB)
            lower = left[:, there].T
            work[there, :] -= jnp.dot(lower, left[...], precision=lax.Precision.HIGHEST)
            out_ref[there, :] -= jnp.dot(lower, right[...], precision=lax.Precision.HIGHEST)
            return carry

        return lax.fori_loop(k + 1, blocks, update, carry)

    lax.fori_loop(0, blocks, step, 0)


def cholesky_inverse(gram):
    size = gram.shape[0]
    return pl.pallas_call(
        cholesky_inverse_kernel,
        out_shape=jax.ShapeDtypeStruct((size, size), jnp.float32),
        in_specs=[pl.BlockSpec(memory_space=pltpu.VMEM)],
        out_specs=pl.BlockSpec(memory_space=pltpu.VMEM),
        scratch_shapes=[
            pltpu.VMEM((size, size), jnp.float32),
            pltpu.VMEM((NB, size), jnp.float32),
            pltpu.VMEM((NB, size), jnp.float32),
        ],
        compiler_params=pltpu.CompilerParams(vmem_limit_bytes=24 << 20),
        cost_estimate=pl.CostEstimate(
            flops=100_000_000_000, bytes_accessed=2 * size * size * 4, transcendentals=0
        ),
    )(gram)


def quantize(value, group):
    height, width = value.shape
    grouped = value.reshape(height // group, group, width)
    top = jnp.max(jnp.abs(grouped), axis=1, keepdims=True)
    factor = jnp.where(top > 1e-30, LEVELS / jnp.maximum(top, 1e-30), 0.0)
    code = jnp.round(grouped * factor).astype(jnp.int16).reshape(height, width)
    return code, top.reshape(height // group, width) * (1.0 / LEVELS)


def dequantize(code, scale, group):
    height, width = code.shape
    grouped = code.astype(jnp.float32).reshape(height // group, group, width)
    return (grouped * scale[:, None, :]).reshape(height, width)


def send(value, bit):
    size = lax.axis_size("arc")
    return lax.ppermute(value, "arc", [(i, i ^ bit) for i in range(size)])


def send_coded(value, bit):
    code, scale = quantize(value, GROUP)
    return dequantize(send(code, bit), send(scale, bit), GROUP)


def on_device_paired(design, arc_lengths, kaula_prior):
    obs_dev, ord_cols = design.shape
    arcs = lax.axis_size("arc")
    slab_rows = TILE * PANELS
    width = ord_cols // arcs
    me = lax.axis_index("arc")
    core, x, z = me % 2, (me // 2) % 2, me // 4
    inverse_norm = 1.0 / math.sqrt(arcs * obs_dev)
    dims = (((0,), (0,)), ((), ()))

    def product(a, b):
        return lax.dot_general(a, b, dims, preferred_element_type=jnp.float32)

    slab = design[:, :slab_rows]
    arrived = lax.ppermute(slab, "ord", [(0, 1)])
    slab = jnp.where(lax.axis_index("ord") == 0, slab, arrived)
    position = lax.broadcasted_iota(jnp.int32, (obs_dev, 1), 0)
    masked = jnp.where(position < arc_lengths[0], slab, jnp.zeros((), slab.dtype))

    def pair(k, c):
        parts = []
        for flip in range(2):
            block = ((z ^ k) * 2 + (x ^ flip)) * 2 + c
            parts.append(lax.dynamic_slice(design, (0, block * width), (obs_dev, width)))
        return jnp.concatenate(parts, axis=1)

    others = {k: send(pair(k, 1 - core), 1) for k in (3, 2, 1, 0)}
    masked_other = send(masked, 1)

    gram = lax.psum_scatter(product(masked, slab), "arc", scatter_dimension=0, tiled=True)
    gram = lax.all_gather(gram, "arc", axis=0, tiled=True) * inverse_norm
    row_ids = lax.broadcasted_iota(jnp.int32, (slab_rows, slab_rows), 0)
    col_ids = lax.broadcasted_iota(jnp.int32, (slab_rows, slab_rows), 1)
    gram = gram + jnp.where(row_ids == col_ids, kaula_prior[:, None], 0.0)
    inverse = cholesky_inverse(gram)

    sums = {}
    for k in (3, 2, 1, 0):
        part = product(masked, pair(k, core)) + product(masked_other, others[k])
        sums[k] = part[:, :width] + send_coded(part[:, width:], 2)
        if k == 3:
            from_three = send_coded(sums[3], 4)
        if k == 2:
            from_two = send_coded(sums[2] + from_three, 8)
        if k == 1:
            from_one = send_coded(sums[1], 4)
    matrix = (sums[0] + from_one + from_two) * inverse_norm
    holds_gram = (lax.axis_index("ord") == 0) & (me == 0)
    matrix = jnp.where(holds_gram, gram, matrix)
    share = jnp.dot(inverse, matrix, precision=lax.Precision.HIGHEST)
    group = slab_rows // arcs
    code, scale = quantize(share, group)
    code = lax.all_to_all(code, "arc", split_axis=0, concat_axis=1, tiled=True)
    scale = lax.all_to_all(scale, "arc", split_axis=0, concat_axis=1, tiled=True)
    return code.astype(jnp.float32) * scale


def solution(mesh):
    in_specs = (P("arc", "ord"), P("arc"), P())
    out_specs = P("arc", "ord")
    paired = mesh.shape["arc"] == 16 and mesh.shape["ord"] == 2
    return jax.shard_map(
        on_device_paired if paired else on_device,
        mesh=mesh, in_specs=in_specs, out_specs=out_specs, check_vma=False
    )
```
